32 devices in a mesh: slab: 8 (over y, x, core), coil: 4 (over z).
Axes of the slice: x: 2, y: 2, z: 4, core: 2. Of those that a mesh axis runs over, the one named last changes fastest.
Arguments:
- sensitivity: float32 [4, 2, 16, 256, 128], P('coil', None, 'slab'), may hold values from -4 to 4
- kspace: float32 [4, 2, 16, 256, 128], P('coil', None, 'slab')
- sampling: int32 [16, 256, 128], P('slab'), may hold values 0 or 1
- prior_image: float32 [2, 16, 256, 128], P(None, 'slab', 'coil')
- w_first: bfloat16 [32, 2, 3, 3, 3], replicated, may hold values from -0.875 to 0.875
- w_middle: bfloat16 [3, 32, 32, 3, 3, 3], replicated, may hold values from -0.21875 to 0.21875
- w_last: bfloat16 [2, 32, 3, 3, 3], replicated, may hold values from -0.21875 to 0.21875
Outputs:
- solution: float32 [2, 16, 256, 128], P(None, 'slab', 'coil')
- refined: float32 [2, 16, 256, 128], P(None, 'slab', 'coil')
The draws below stay inside these ranges and needn't reach their ends.
Inputs may be any that keep to these rules, and one draw needn't show every extreme that they name: sampling marks the measured ky-kz positions of each readout plane.
All inputs are finite; a program needn't handle non-finite values. No bound on the sum of `sampling` on one device may be relied on, other than what follows from the above.
Results may differ from the reference program's by a relative error of at most 0.0015.
Values may be sent and summed in bfloat16 or wider, within the bound.
A program may use at most 128 MiB of HBM per device.

```python
import math
import jax
import jax.numpy as jnp
from jax import lax

NY = 256
NZ = 128
CHANNELS = 32
LAYERS = 5
ITERS = 2
NX = 16
COILS = 4


def scaled_field(key, lead_shape):
    full_shape = lead_shape + (NX, NY, NZ)
    key_values, key_rows, key_columns = jax.random.split(key, 3)
    positions = jnp.arange(NX, dtype=jnp.float32) / max(NX - 1, 1)
    values_raw = jax.random.truncated_normal(key_values, -4.0, 4.0, full_shape, jnp.float32)
    ramp_x = 3.0 ** (0.5 * positions)
    log_half = 0.5 * math.log(10.0)
    row_scale = jnp.exp(jax.random.uniform(key_rows, (NY,), jnp.float32, -log_half, log_half))
    column_scale = jnp.exp(jax.random.uniform(key_columns, (NZ,), jnp.float32, -log_half, log_half))
    return values_raw * ramp_x[:, None, None] * row_scale[:, None] * column_scale


def draw_kspace(key, part):
    return scaled_field(jax.random.fold_in(key, 11), (COILS, 2))


def draw_prior_image(key, part):
    return scaled_field(jax.random.fold_in(key, 23), (2,))


def touch_ends(values, own_key, low, largest):
    dims = values.shape
    spot = [jax.random.randint(jax.random.fold_in(own_key, axis), (), 0, dims[axis]) for axis in range(len(dims))]
    values = values.at[tuple(spot)].set(low)
    longest = dims.index(max(dims))
    spot[longest] = (spot[longest] + 1) % dims[longest]
    return values.at[tuple(spot)].set(largest)


def steps_of(key, shape, cuts, smallest, high):
    level = 1.0
    for dim, shards_of in cuts:
        draws = jax.random.uniform(jax.random.fold_in(jax.random.fold_in(key, 6), dim), (shards_of,), jnp.float32, smallest / len(cuts), high / len(cuts))
        level = level * jnp.repeat(jnp.exp(draws), shape[dim] // shards_of).reshape((-1,) + (1,) * (len(shape) - 1 - dim))
    return level


def normal_values(rng, dims, spread, limit, cuts=(), kind=jnp.bfloat16):
    entries = jax.random.normal(rng, dims, jnp.float32) * spread
    if len(cuts) > 0:
        entries = steps_of(rng, dims, cuts, -0.22, 0.18) * entries
    return jnp.clip(entries, min=-limit, max=limit).astype(kind)


def setup_inputs(seed: int = 0) -> dict:
    key_of = jax.random.split(jax.random.key(seed), 8)
    return {
        "sensitivity": normal_values(key_of[0], (COILS, 2, NX, NY, NZ), ((2 * COILS) ** -0.5), 4.0, ((0, 4), (2, 8)), jnp.float32),
        "kspace": draw_kspace(jax.random.fold_in(key_of[7], 71), 0),
        "sampling": touch_ends((jax.random.randint(key_of[2], (NX, NY, NZ), 0, 3) < 1).astype(jnp.int32), jax.random.fold_in(key_of[2], 1), 0, 1),
        "prior_image": draw_prior_image(jax.random.fold_in(key_of[7], 71), 0),
        "w_first": normal_values(key_of[4], (CHANNELS, 2, 3, 3, 3), 54 ** -0.5, 0.875),
        "w_middle": normal_values(key_of[5], (LAYERS - 2, CHANNELS, CHANNELS, 3, 3, 3), (27 * CHANNELS) ** -0.5, 0.21875),
        "w_last": normal_values(key_of[6], (2, CHANNELS, 3, 3, 3), (27 * CHANNELS) ** -0.5, 0.21875),
    }


LAMBDA = 0.5


def to_kspace(field):
    values = jnp.fft.fft2(lax.complex(field[0], field[1]), axes=(-2, -1), norm="ortho")
    return jnp.stack([jnp.real(values), jnp.imag(values)])


def to_image(field):
    values = jnp.fft.ifft2(lax.complex(field[0], field[1]), axes=(-2, -1), norm="ortho")
    return jnp.stack([jnp.real(values), jnp.imag(values)])


def conj_apply(coil_maps, field):
    real_part = coil_maps[0] * field[0] + coil_maps[1] * field[1]
    imag_part = coil_maps[0] * field[1] - coil_maps[1] * field[0]
    return jnp.stack([real_part, imag_part])


def normal_image(direction, sensitivity, mask_f):
    def one_coil(total, coil_maps):
        coil_field = jnp.stack([coil_maps[0] * direction[0] - coil_maps[1] * direction[1],
                                coil_maps[0] * direction[1] + coil_maps[1] * direction[0]])
        spectrum = to_kspace(coil_field) * mask_f
        return total + conj_apply(coil_maps, to_image(spectrum)), None

    total, _ = lax.scan(one_coil, jnp.zeros_like(direction), sensitivity)
    return total


def adjoint_image(sensitivity, kspace, mask_f, template):
    def one_coil(total, pieces):
        coil_maps, measured = pieces
        return total + conj_apply(coil_maps, to_image(measured * mask_f)), None

    total, _ = lax.scan(one_coil, jnp.zeros_like(template), (sensitivity, kspace))
    return total


def conv_volume(activation, weight):
    result = lax.conv_general_dilated(activation[None].astype(jnp.float32), weight.astype(jnp.float32),
                                      (1, 1, 1), "SAME", dimension_numbers=("NCDHW", "OIDHW", "NCDHW"),
                                      precision=lax.Precision.HIGHEST)
    return result[0]


def reference(sensitivity, kspace, sampling, prior_image, w_first, w_middle, w_last):
    mask_f = sampling.astype(jnp.float32)
    rhs = adjoint_image(sensitivity, kspace, mask_f, prior_image) + LAMBDA * prior_image
    solution = jnp.zeros_like(prior_image)
    residual = rhs
    direction = rhs
    norm_now = jnp.sum(residual * residual)
    for step_index in range(ITERS):
        image_q = normal_image(direction, sensitivity, mask_f) + LAMBDA * direction
        step_size = norm_now / jnp.sum(direction * image_q)
        solution = solution + step_size * direction
        if step_index + 1 < ITERS:
            residual = residual - step_size * image_q
            norm_next = jnp.sum(residual * residual)
            direction = residual + (norm_next / norm_now) * direction
            norm_now = norm_next
    features = solution.astype(jnp.bfloat16)
    hidden = jax.nn.relu(conv_volume(features, w_first)).astype(jnp.bfloat16)
    for layer_index in range(w_middle.shape[0]):
        hidden = jax.nn.relu(conv_volume(hidden, w_middle[layer_index])).astype(jnp.bfloat16)
    correction = conv_volume(hidden, w_last)
    return solution, solution + correction
```

```python
import functools
import math

import jax
import jax.numpy as jnp
from jax import lax
from jax.experimental import pallas as pl
from jax.experimental.pallas import tpu as pltpu
from jax.sharding import PartitionSpec as P

ITERS = 2


LAMBDA = 0.5
HIGHEST = lax.Precision.HIGHEST


def dft_tables(length, sign):
    positions = jnp.arange(length, dtype=jnp.int32)
    phases = positions[:, None] * positions[None, :] % length
    angles = 2.0 * math.pi / length * phases.astype(jnp.float32)
    scaling = 1.0 / math.sqrt(length)
    return (jnp.cos(angles) * scaling, sign * scaling * jnp.sin(angles))


def transform(field, tables):
    cosine_y, sine_y, cosine_z, sine_z = tables
    plain = jnp.einsum("ky,acpyz->acpkz", cosine_y, field, precision=HIGHEST)
    turned = jnp.einsum("ky,acpyz->acpkz", sine_y, field, precision=HIGHEST)
    field = jnp.stack([plain[0] - turned[1], plain[1] + turned[0]])
    plain = jnp.einsum("acpyz,zk->acpyk", field, cosine_z, precision=HIGHEST)
    turned = jnp.einsum("acpyz,zk->acpyk", field, sine_z, precision=HIGHEST)
    return jnp.stack([plain[0] - turned[1], plain[1] + turned[0]])


def combine_coils(field, coil_maps):
    real_part = jnp.sum(coil_maps[0] * field[0] + coil_maps[1] * field[1], axis=0)
    imag_part = jnp.sum(coil_maps[0] * field[1] - coil_maps[1] * field[0], axis=0)
    return jnp.stack([real_part, imag_part])


def coil_terms(image, coil_maps, mask_f, forward, backward):
    image_re = image[0][None]
    image_im = image[1][None]
    coil_field = jnp.stack(
        [
            coil_maps[0] * image_re - coil_maps[1] * image_im,
            coil_maps[0] * image_im + coil_maps[1] * image_re,
        ]
    )
    spectrum = transform(coil_field, forward) * mask_f
    energy = jnp.sum(spectrum * spectrum)
    return (combine_coils(transform(spectrum, backward), coil_maps), energy)


def coil_total(local_image):
    return lax.psum(local_image, "coil")


def image_total(value):
    return lax.psum(value, "slab")


def curvature(direction, energy):
    weight_share = LAMBDA / lax.axis_size("coil")
    local_sum = energy + weight_share * jnp.sum(direction * direction)
    return lax.psum(local_sum, ("slab", "coil"))


def block_weights(weight, x_outs, y_outs, in_pad, out_pad):
    weight = jnp.pad(weight, ((0, out_pad), (0, in_pad), (0, 0), (0, 0), (0, 0)))
    weight = jnp.transpose(weight, (4, 0, 3, 2, 1))
    parts = []
    for x_out in range(x_outs):
        for y_out in range(y_outs):
            spread = ((0, 0), (0, 0), (y_out, y_outs - 1 - y_out), (x_out, x_outs - 1 - x_out), (0, 0))
            parts.append(jnp.pad(weight, spread))
    stacked = jnp.stack(parts)
    return stacked.reshape(stacked.shape[0] * stacked.shape[1] * stacked.shape[2], -1)


def conv_rows(weight_ref, source, sink, rows, planes, x_outs, y_outs, group, top, height, last):
    width = source.shape[-1]
    channels = source.shape[2]
    weight_rows = weight_ref.shape[0]
    outs = weight_rows // (3 * x_outs * y_outs)
    lanes = lax.broadcasted_iota(jnp.int32, (outs, width), 1)
    depth = (y_outs + 2) * (x_outs + 2) * channels

    def step(index, carry):
        y = index * y_outs
        for first in range(0, planes, x_outs * group):
            blocks = [
                source[pl.ds(y, y_outs + 2), first + k * x_outs : first + (k + 1) * x_outs + 2].reshape(depth, width)
                for k in range(group)
            ]
            taken = jnp.concatenate(blocks, axis=1) if group > 1 else blocks[0]
            product = jnp.dot(weight_ref[...], taken, preferred_element_type=jnp.float32)
            for x_out in range(x_outs):
                for y_out in range(y_outs):
                    base = (x_out * y_outs + y_out) * 3 * outs
                    y_now = y + y_out
                    inside = jnp.logical_and(top + y_now >= 0, top + y_now < height)
                    for k in range(group):
                        span = slice(k * width, (k + 1) * width)
                        before = product[base : base + outs, span]
                        centre = product[base + outs : base + 2 * outs, span]
                        after = product[base + 2 * outs : base + 3 * outs, span]
                        before = jnp.where(lanes == 0, 0.0, pltpu.roll(before, 1, 1))
                        after = jnp.where(lanes == width - 1, 0.0, pltpu.roll(after, width - 1, 1))
                        value = centre + before + after
                        plane = first + k * x_outs + x_out
                        if last:
                            sink[y_now, plane] = value
                        else:
                            value = jnp.where(inside, jnp.maximum(value, 0.0), 0.0)
                            sink[y_now, plane + 1] = value.astype(jnp.bfloat16)
        return carry

    lax.fori_loop(0, rows // y_outs, step, 0)


def denoise_kernel(x_outs, y_outs, group, rows, block_rows, height, features, first, middle, final, out, even, odd):
    planes = features.shape[1] - 2
    layers = middle.shape[0] + 2
    top = lax.axis_index("coil") * block_rows + lax.axis_index("slab") * rows
    buffers = (even, odd)
    for buffer in buffers:
        edge = jnp.zeros((buffer.shape[0],) + buffer.shape[2:], buffer.dtype)
        buffer[:, 0] = edge
        buffer[:, planes + 1] = edge
    shared = (planes, x_outs, y_outs, group)
    left = layers - 1
    conv_rows(first, features, even, rows + 2 * left, *shared, top - left, height, False)
    for layer in range(layers - 2):
        left = left - 1
        conv_rows(
            middle.at[layer], buffers[layer % 2], buffers[(layer + 1) % 2],
            rows + 2 * left, *shared, top - left, height, False,
        )
    conv_rows(final, buffers[(layers - 2) % 2], out, rows, *shared, top, height, True)


def denoise(features, w_first, w_middle, w_last, rows, block_rows, height):
    planes = features.shape[1]
    width = features.shape[3]
    channels = w_first.shape[0]
    layers = w_middle.shape[0] + 2
    x_outs = 2 if planes % 2 == 0 else 1
    y_outs = 2 if rows % 2 == 0 else 1
    group = 2 if (planes // x_outs) % 2 == 0 else 1
    in_rows = 16
    features = jnp.pad(features, ((0, 0), (1, 1), (0, in_rows - features.shape[2]), (0, 0)))
    first = block_weights(w_first, x_outs, y_outs, in_rows - w_first.shape[1], 0)
    middle = jnp.stack([block_weights(w_middle[m], x_outs, y_outs, 0, 0) for m in range(layers - 2)])
    final = block_weights(w_last, x_outs, y_outs, 0, -w_last.shape[0] % 8)
    outs = w_last.shape[0]
    held = (rows + 2 * (layers - 1), planes + 2, channels, width)
    result = pl.pallas_call(
        functools.partial(denoise_kernel, x_outs, y_outs, group, rows, block_rows, height),
        out_shape=jax.ShapeDtypeStruct((rows, planes, outs + -outs % 8, width), jnp.float32),
        in_specs=[pl.BlockSpec(memory_space=pltpu.VMEM)] * 4,
        out_specs=pl.BlockSpec(memory_space=pltpu.VMEM),
        scratch_shapes=[pltpu.VMEM(held, jnp.bfloat16), pltpu.VMEM(held, jnp.bfloat16)],
        compiler_params=pltpu.CompilerParams(vmem_limit_bytes=48 * 1024 * 1024),
    )(features, first, middle, final)
    return result[:, :, :outs]


def body(sensitivity, kspace, sampling, prior_image, w_first, w_middle, w_last):
    coil_maps = jnp.moveaxis(sensitivity, 1, 0)
    measured = jnp.moveaxis(kspace, 1, 0)
    mask_f = sampling.astype(jnp.float32)
    len_y = coil_maps.shape[3]
    len_z = coil_maps.shape[4]
    forward = dft_tables(len_y, -1.0) + dft_tables(len_z, -1.0)
    backward = dft_tables(len_y, 1.0) + dft_tables(len_z, 1.0)
    block_rows = prior_image.shape[2]
    prior_view = lax.all_gather(prior_image, "coil", axis=2, tiled=True)
    adjoint_local = combine_coils(transform(measured * mask_f, backward), coil_maps)
    rhs = coil_total(adjoint_local) + LAMBDA * prior_view
    solution = jnp.zeros_like(rhs)
    residual = rhs
    direction = rhs
    norm_now = image_total(jnp.sum(residual * residual))
    for step_index in range(ITERS):
        local_q, energy = coil_terms(direction, coil_maps, mask_f, forward, backward)
        image_q = coil_total(local_q) + LAMBDA * direction
        step_size = norm_now / curvature(direction, energy)
        solution = solution + step_size * direction
        if step_index + 1 < ITERS:
            residual = residual - step_size * image_q
            norm_next = image_total(jnp.sum(residual * residual))
            direction = residual + norm_next / norm_now * direction
            norm_now = norm_next
    brick = lax.dynamic_slice_in_dim(solution, lax.axis_index("coil") * block_rows, block_rows, 2)
    halo = w_middle.shape[0] + 2
    shares = lax.axis_size("slab")
    rows = block_rows // shares
    padded = jnp.pad(solution.astype(jnp.bfloat16), ((0, 0), (0, 0), (halo, halo), (0, 0)))
    mine = lax.dynamic_slice_in_dim(padded, lax.axis_index("coil") * block_rows, block_rows + 2 * halo, 2)
    mine = jnp.transpose(mine, (2, 1, 0, 3))
    pieces = jnp.stack([mine[s * rows : (s + 1) * rows + 2 * halo] for s in range(shares)])
    taken = lax.all_to_all(pieces, "slab", 0, 0)
    features = jnp.moveaxis(taken, 0, 1).reshape((rows + 2 * halo, -1) + taken.shape[3:])
    correction = denoise(features, w_first, w_middle, w_last, rows, block_rows, len_y)
    local = prior_image.shape[1]
    pieces = jnp.moveaxis(correction.reshape((rows, shares, local) + correction.shape[2:]), 1, 0)
    taken = lax.all_to_all(pieces, "slab", 0, 0)
    correction = jnp.transpose(taken.reshape((block_rows,) + taken.shape[2:]), (2, 1, 0, 3))
    return (brick, brick + correction)


def solution(mesh):
    placed = (
        P("coil", None, "slab", None, None),
        P("coil", None, "slab", None, None),
        P("slab", None, None),
        P(None, "slab", "coil", None),
        P(),
        P(),
        P(),
    )
    return jax.shard_map(
        body,
        mesh=mesh,
        in_specs=placed,
        out_specs=(P(None, "slab", "coil", None), P(None, "slab", "coil", None)),
        check_vma=False,
    )
```

```python
import functools

import jax
import jax.numpy as jnp
import numpy as np
from jax import lax
from jax.experimental import pallas as pl
from jax.experimental.pallas import tpu as pltpu
from jax.sharding import PartitionSpec as P

LAMBDA = 0.5
MESH = pl.DeviceIdType.MESH


def dft_parts(length):
    positions = np.arange(length)
    angles = 2.0 * np.pi / length * (positions[:, None] * positions[None, :] % length)
    return np.cos(angles) / np.sqrt(length), np.sin(angles) / np.sqrt(length)


def halves(table):
    table = table.astype(np.float32)
    high = table.astype(jnp.bfloat16)
    low = (table - high.astype(np.float32)).astype(jnp.bfloat16)
    return jnp.asarray(high), jnp.asarray(low)


def split(values):
    high = values.astype(jnp.bfloat16)
    return high, (values - high.astype(jnp.float32)).astype(jnp.bfloat16)


def multiply(left, right):
    return jnp.dot(left, right, preferred_element_type=jnp.float32)


def transform(real, imag, y_high, y_low, z_high, z_low):
    planes = len(real)
    rows, width = real[0].shape
    field = jnp.concatenate([jnp.concatenate(real, axis=1), jnp.concatenate(imag, axis=1)], axis=0)
    high, low = split(field)
    both = multiply(y_high[...], jnp.concatenate([high, low], axis=1))
    span = planes * width
    field = both[:, :span] + both[:, span:] + multiply(y_low[...], high)
    field = jnp.concatenate(
        [
            jnp.concatenate([field[:rows, p * width : (p + 1) * width], field[rows:, p * width : (p + 1) * width]], axis=1)
            for p in range(planes)
        ],
        axis=0,
    )
    high, low = split(field)
    both = multiply(jnp.concatenate([high, low], axis=0), z_high[...])
    span = planes * rows
    field = both[:span] + both[span:] + multiply(high, z_low[...])
    pieces = [field[p * rows : (p + 1) * rows] for p in range(planes)]
    return [piece[:, :width] for piece in pieces], [piece[:, width:] for piece in pieces]


def total_of(values):
    return jnp.sum(jnp.sum(values, axis=0, keepdims=True), axis=1, keepdims=True)


def gradients_kernel(
    shares, coils, maps, measured, mask, prior, y_high, y_low, z_high, z_low,
    out, part, arrived, rhs, spectrum, own_residual, residual, note, notes,
    block_send, block_recv, note_send, note_recv,
):
    slab = lax.axis_index("slab")
    coil = lax.axis_index("coil")
    devices = shares * coils
    me = slab * coils + coil
    planes = maps.shape[1]
    block = prior.shape[2]
    tables = (y_high, y_low, z_high, z_low)

    def device_at(distance):
        other = lax.rem(me + distance, devices)
        return (other // coils, lax.rem(other, coils))

    barrier = pltpu.get_barrier_semaphore()
    for distance in range(1, devices):
        pl.semaphore_signal(barrier, inc=1, device_id=device_at(distance), device_id_type=MESH)
    pl.semaphore_wait(barrier, devices - 1)

    def rows_of(index):
        return pl.ds(pl.multiple_of(index * block, block), block)

    mine = rows_of(coil)

    def scatter(phase):
        copies = []
        for distance in range(1, coils):
            target = lax.rem(coil + distance, coils)
            copies.append(
                pltpu.make_async_remote_copy(
                    src_ref=part.at[phase, :, :, rows_of(target)],
                    dst_ref=arrived.at[phase, distance - 1],
                    send_sem=block_send.at[2 * phase, distance - 1],
                    recv_sem=block_recv.at[2 * phase, distance - 1],
                    device_id=(slab, target),
                    device_id_type=MESH,
                )
            )
        for copy in copies:
            copy.start()
        return copies

    def gather(buffer, phase):
        copies = []
        for distance in range(1, coils):
            copies.append(
                pltpu.make_async_remote_copy(
                    src_ref=buffer.at[:, :, mine],
                    dst_ref=buffer.at[:, :, mine],
                    send_sem=block_send.at[2 * phase + 1, distance - 1],
                    recv_sem=block_recv.at[2 * phase + 1, distance - 1],
                    device_id=(slab, lax.rem(coil + distance, coils)),
                    device_id_type=MESH,
                )
            )
        for copy in copies:
            copy.start()
        return copies

    def tell(phase):
        copies = []
        for distance in range(1, devices):
            copies.append(
                pltpu.make_async_remote_copy(
                    src_ref=note.at[phase],
                    dst_ref=notes.at[phase, distance - 1],
                    send_sem=note_send.at[phase, distance - 1],
                    recv_sem=note_recv.at[phase, distance - 1],
                    device_id=device_at(distance),
                    device_id_type=MESH,
                )
            )
        for copy in copies:
            copy.start()
        return copies

    def finish(copies):
        for copy in copies:
            copy.wait()

    lanes = lax.broadcasted_iota(jnp.int32, (1, note.shape[2]), 1)

    def write_note(phase, values):
        line = jnp.zeros(lanes.shape, jnp.float32)
        for index, value in enumerate(values):
            line = jnp.where(lanes == index, value, line)
        note[phase] = line

    def read_notes(phase, count):
        line = note[phase]
        for distance in range(1, devices):
            line = line + notes[phase, distance - 1]
        return [jnp.sum(jnp.where(lanes == index, line, 0.0), axis=1, keepdims=True) for index in range(count)]

    def backward_part(real, imag, phase):
        imag, real = transform(imag, real, *tables)
        for p in range(planes):
            part[phase, 0, p] = maps[0, p] * real[p] + maps[1, p] * imag[p]
            part[phase, 1, p] = maps[0, p] * imag[p] - maps[1, p] * real[p]

    def forward(image):
        real = [maps[0, p] * image(0, p) - maps[1, p] * image(1, p) for p in range(planes)]
        imag = [maps[0, p] * image(1, p) + maps[1, p] * image(0, p) for p in range(planes)]
        real, imag = transform(real, imag, *tables)
        sampled = [mask[p].astype(jnp.float32) for p in range(planes)]
        return [[real[p] * sampled[p] for p in range(planes)], [imag[p] * sampled[p] for p in range(planes)]]

    def reduced(phase, h, p):
        value = part[phase, h, p, mine]
        for distance in range(1, coils):
            value = value + arrived[phase, distance - 1, h, p]
        return value

    sampled = [mask[p].astype(jnp.float32) for p in range(planes)]
    backward_part(
        [measured[0, p] * sampled[p] for p in range(planes)], [measured[1, p] * sampled[p] for p in range(planes)], 0
    )
    finish(scatter(0))
    entries = [(h, p) for h in range(2) for p in range(planes)]
    for h, p in entries:
        rhs[h, p, mine] = reduced(0, h, p) + LAMBDA * prior[h, p]
    finish(gather(rhs, 0))

    norm = jnp.zeros((1, 1), jnp.float32)
    for h, p in entries:
        value = rhs[h, p, mine]
        norm = norm + total_of(value * value)
    result = forward(lambda h, p: rhs[h, p])
    energy = LAMBDA * norm
    for h, p in entries:
        spectrum[h, p] = result[h][p]
        energy = energy + total_of(result[h][p] * result[h][p])
    write_note(0, [norm, energy])
    first_notes = tell(0)
    backward_part([spectrum[0, p] for p in range(planes)], [spectrum[1, p] for p in range(planes)], 1)
    second_parts = scatter(1)
    finish(first_notes)
    norm, curvature = read_notes(0, 2)
    step = norm / curvature
    finish(second_parts)
    norm_next = jnp.zeros((1, 1), jnp.float32)
    cross = jnp.zeros((1, 1), jnp.float32)
    for h, p in entries:
        direction = rhs[h, p, mine]
        value = direction - step * (reduced(1, h, p) + LAMBDA * direction)
        own_residual[h, p] = value
        residual[h, p, mine] = value.astype(jnp.bfloat16)
        norm_next = norm_next + total_of(value * value)
        cross = cross + LAMBDA * total_of(value * direction)
    finish(gather(residual, 1))
    result = forward(lambda h, p: residual[h, p].astype(jnp.float32))
    energy = LAMBDA * norm_next
    for h, p in entries:
        energy = energy + total_of(result[h][p] * result[h][p])
        cross = cross + total_of(result[h][p] * spectrum[h, p])
    write_note(1, [norm_next, energy, cross])
    finish(tell(1))
    norm_next, energy, cross = read_notes(1, 3)
    ratio = norm_next / norm
    curvature = energy + 2.0 * ratio * cross + ratio * ratio * curvature
    step_next = norm_next / curvature
    for h, p in entries:
        direction = rhs[h, p, mine]
        out[h, p] = step * direction + step_next * (own_residual[h, p] + ratio * direction)


def gradients(maps, measured, mask, prior):
    planes, rows, width = mask.shape
    block = prior.shape[2]
    shares = lax.axis_size("slab")
    coils = lax.axis_size("coil")
    cosine, sine = dft_parts(rows)
    y_tables = halves(np.block([[cosine, sine], [-sine, cosine]]))
    cosine, sine = dft_parts(width)
    z_tables = halves(np.block([[cosine, -sine], [sine, cosine]]))
    image = (2, planes, rows, width)
    brick = (2, planes, block, width)
    return pl.pallas_call(
        functools.partial(gradients_kernel, shares, coils),
        out_shape=jax.ShapeDtypeStruct(brick, jnp.float32),
        in_specs=[pl.BlockSpec(memory_space=pltpu.VMEM)] * 8,
        out_specs=pl.BlockSpec(memory_space=pltpu.VMEM),
        scratch_shapes=[
            pltpu.VMEM((2,) + image, jnp.float32),
            pltpu.VMEM((2, coils - 1) + brick, jnp.float32),
            pltpu.VMEM(image, jnp.float32),
            pltpu.VMEM(image, jnp.float32),
            pltpu.VMEM(brick, jnp.float32),
            pltpu.VMEM(image, jnp.bfloat16),
            pltpu.VMEM((2, 1, 128), jnp.float32),
            pltpu.VMEM((2, shares * coils - 1, 1, 128), jnp.float32),
            pltpu.SemaphoreType.DMA((4, coils - 1)),
            pltpu.SemaphoreType.DMA((4, coils - 1)),
            pltpu.SemaphoreType.DMA((2, shares * coils - 1)),
            pltpu.SemaphoreType.DMA((2, shares * coils - 1)),
        ],
        compiler_params=pltpu.CompilerParams(
            collective_id=0, has_side_effects=True, vmem_limit_bytes=56 * 1024 * 1024
        ),
    )(maps, measured, mask, prior, *y_tables, *z_tables)


def row_halo(cells, width):
    count = lax.axis_size("coil")
    tail = cells[:, :, cells.shape[2] - width :]
    head = cells[:, :, :width]
    return jnp.concatenate(
        [
            lax.ppermute(tail, "coil", [(i, i + 1) for i in range(count - 1)]),
            cells,
            lax.ppermute(head, "coil", [(i + 1, i) for i in range(count - 1)]),
        ],
        axis=2,
    )


def block_weights(weight, x_outs, y_outs, in_pad, out_pad):
    weight = jnp.pad(weight, ((0, out_pad), (0, in_pad), (0, 0), (0, 0), (0, 0)))
    weight = jnp.transpose(weight, (4, 0, 3, 2, 1))
    parts = []
    for x_out in range(x_outs):
        for y_out in range(y_outs):
            spread = ((0, 0), (0, 0), (y_out, y_outs - 1 - y_out), (x_out, x_outs - 1 - x_out), (0, 0))
            parts.append(jnp.pad(weight, spread))
    stacked = jnp.stack(parts)
    return stacked.reshape(stacked.shape[0] * stacked.shape[1] * stacked.shape[2], -1)


def conv_rows(weight_ref, source, sink, rows, planes, x_outs, y_outs, group, top, height, last):
    width = source.shape[-1]
    channels = source.shape[2]
    weight_rows = weight_ref.shape[0]
    outs = weight_rows // (3 * x_outs * y_outs)
    lanes = lax.broadcasted_iota(jnp.int32, (outs, width), 1)
    depth = (y_outs + 2) * (x_outs + 2) * channels

    def step(index, carry):
        y = index * y_outs
        for first in range(0, planes, x_outs * group):
            blocks = [
                source[pl.ds(y, y_outs + 2), first + k * x_outs : first + (k + 1) * x_outs + 2].reshape(depth, width)
                for k in range(group)
            ]
            taken = jnp.concatenate(blocks, axis=1) if group > 1 else blocks[0]
            product = jnp.dot(weight_ref[...], taken, preferred_element_type=jnp.float32)
            for x_out in range(x_outs):
                for y_out in range(y_outs):
                    base = (x_out * y_outs + y_out) * 3 * outs
                    y_now = y + y_out
                    inside = jnp.logical_and(top + y_now >= 0, top + y_now < height)
                    for k in range(group):
                        span = slice(k * width, (k + 1) * width)
                        before = product[base : base + outs, span]
                        centre = product[base + outs : base + 2 * outs, span]
                        after = product[base + 2 * outs : base + 3 * outs, span]
                        before = jnp.where(lanes == 0, 0.0, pltpu.roll(before, 1, 1))
                        after = jnp.where(lanes == width - 1, 0.0, pltpu.roll(after, width - 1, 1))
                        value = centre + before + after
                        plane = first + k * x_outs + x_out
                        if last:
                            sink[y_now, plane] = value
                        else:
                            value = jnp.where(inside, jnp.maximum(value, 0.0), 0.0)
                            sink[y_now, plane + 1] = value.astype(jnp.bfloat16)
        return carry

    lax.fori_loop(0, rows // y_outs, step, 0)


def denoise_kernel(x_outs, y_outs, group, rows, block_rows, height, features, first, middle, final, out, even, odd):
    planes = features.shape[1] - 2
    layers = middle.shape[0] + 2
    top = lax.axis_index("coil") * block_rows + lax.axis_index("slab") * rows
    buffers = (even, odd)
    for buffer in buffers:
        edge = jnp.zeros((buffer.shape[0],) + buffer.shape[2:], buffer.dtype)
        buffer[:, 0] = edge
        buffer[:, planes + 1] = edge
    shared = (planes, x_outs, y_outs, group)
    left = layers - 1
    conv_rows(first, features, even, rows + 2 * left, *shared, top - left, height, False)
    for layer in range(layers - 2):
        left = left - 1
        conv_rows(
            middle.at[layer], buffers[layer % 2], buffers[(layer + 1) % 2],
            rows + 2 * left, *shared, top - left, height, False,
        )
    conv_rows(final, buffers[(layers - 2) % 2], out, rows, *shared, top, height, True)


def denoise(features, w_first, w_middle, w_last, rows, block_rows, height):
    planes = features.shape[1]
    width = features.shape[3]
    channels = w_first.shape[0]
    layers = w_middle.shape[0] + 2
    x_outs = 2 if planes % 2 == 0 else 1
    y_outs = 2 if rows % 2 == 0 else 1
    group = 2 if (planes // x_outs) % 2 == 0 else 1
    in_rows = 16
    features = jnp.pad(features, ((0, 0), (1, 1), (0, in_rows - features.shape[2]), (0, 0)))
    first = block_weights(w_first, x_outs, y_outs, in_rows - w_first.shape[1], 0)
    middle = jnp.stack([block_weights(w_middle[m], x_outs, y_outs, 0, 0) for m in range(layers - 2)])
    final = block_weights(w_last, x_outs, y_outs, 0, -w_last.shape[0] % 8)
    outs = w_last.shape[0]
    held = (rows + 2 * (layers - 1), planes + 2, channels, width)
    result = pl.pallas_call(
        functools.partial(denoise_kernel, x_outs, y_outs, group, rows, block_rows, height),
        out_shape=jax.ShapeDtypeStruct((rows, planes, outs + -outs % 8, width), jnp.float32),
        in_specs=[pl.BlockSpec(memory_space=pltpu.VMEM)] * 4,
        out_specs=pl.BlockSpec(memory_space=pltpu.VMEM),
        scratch_shapes=[pltpu.VMEM(held, jnp.bfloat16), pltpu.VMEM(held, jnp.bfloat16)],
        compiler_params=pltpu.CompilerParams(vmem_limit_bytes=48 * 1024 * 1024),
    )(features, first, middle, final)
    return result[:, :, :outs]


def body(sensitivity, kspace, sampling, prior_image, w_first, w_middle, w_last):
    brick = gradients(sensitivity[0], kspace[0], sampling, prior_image)
    len_y = sampling.shape[1]
    block_rows = prior_image.shape[2]
    halo = w_middle.shape[0] + 2
    shares = lax.axis_size("slab")
    rows = block_rows // shares
    mine = row_halo(brick.astype(jnp.bfloat16), halo)
    mine = jnp.transpose(mine, (2, 1, 0, 3))
    pieces = jnp.stack([mine[s * rows : (s + 1) * rows + 2 * halo] for s in range(shares)])
    taken = lax.all_to_all(pieces, "slab", 0, 0)
    features = jnp.moveaxis(taken, 0, 1).reshape((rows + 2 * halo, -1) + taken.shape[3:])
    correction = denoise(features, w_first, w_middle, w_last, rows, block_rows, len_y)
    local = prior_image.shape[1]
    pieces = jnp.moveaxis(correction.reshape((rows, shares, local) + correction.shape[2:]), 1, 0)
    taken = lax.all_to_all(pieces, "slab", 0, 0)
    correction = jnp.transpose(taken.reshape((block_rows,) + taken.shape[2:]), (2, 1, 0, 3))
    return (brick, brick + correction)


def solution(mesh):
    placed = (
        P("coil", None, "slab", None, None),
        P("coil", None, "slab", None, None),
        P("slab", None, None),
        P(None, "slab", "coil", None),
        P(),
        P(),
        P(),
    )
    return jax.shard_map(
        body,
        mesh=mesh,
        in_specs=placed,
        out_specs=(P(None, "slab", "coil", None), P(None, "slab", "coil", None)),
        check_vma=False,
    )
```

```python
import functools

import jax
import jax.numpy as jnp
import numpy as np
from jax import lax
from jax.experimental import pallas as pl
from jax.experimental.pallas import tpu as pltpu
from jax.sharding import PartitionSpec as P

LAMBDA = 0.5
MESH = pl.DeviceIdType.MESH


def dft_parts(length):
    positions = np.arange(length)
    angles = 2.0 * np.pi / length * (positions[:, None] * positions[None, :] % length)
    return np.cos(angles) / np.sqrt(length), np.sin(angles) / np.sqrt(length)


def halves(table):
    table = table.astype(np.float32)
    high = table.astype(jnp.bfloat16)
    low = (table - high.astype(np.float32)).astype(jnp.bfloat16)
    return jnp.asarray(high), jnp.asarray(low)


def split(values):
    high = values.astype(jnp.bfloat16)
    return high, (values - high.astype(jnp.float32)).astype(jnp.bfloat16)


def multiply(left, right):
    return jnp.dot(left, right, preferred_element_type=jnp.float32)


def transform(real, imag, y_high, y_low, z_high, z_low):
    rows, width = real.shape
    high, low = split(jnp.concatenate([real, imag], axis=1))
    both = multiply(y_high[...], jnp.concatenate([high, low], axis=1))
    field = both[:, : 2 * width] + both[:, 2 * width :] + multiply(y_low[...], high)
    field = jnp.concatenate(
        [field[:rows, :width] + field[rows:, width:], field[:rows, width:] - field[rows:, :width]], axis=1
    )
    high, low = split(field)
    both = multiply(jnp.concatenate([high, low], axis=0), z_high[...])
    field = both[:rows] + both[rows:] + multiply(high, z_low[...])
    return field[:, :width], field[:, width:]


def total_of(values):
    return jnp.sum(jnp.sum(values, axis=0, keepdims=True), axis=1, keepdims=True)


def gradients_kernel(
    shares, coils, maps, measured, mask, prior, y_high, y_low, z_high, z_low,
    out, part, arrived, rhs, spectrum, own_residual, residual, note, notes,
    block_send, block_recv, note_send, note_recv,
):
    slab = lax.axis_index("slab")
    coil = lax.axis_index("coil")
    devices = shares * coils
    me = slab * coils + coil
    planes = maps.shape[1]
    block = prior.shape[2]
    tables = (y_high, y_low, z_high, z_low)

    def device_at(distance):
        other = lax.rem(me + distance, devices)
        return (other // coils, lax.rem(other, coils))

    barrier = pltpu.get_barrier_semaphore()
    for distance in range(1, devices):
        pl.semaphore_signal(barrier, inc=1, device_id=device_at(distance), device_id_type=MESH)
    pl.semaphore_wait(barrier, devices - 1)

    def rows_of(index):
        return pl.ds(pl.multiple_of(index * block, block), block)

    mine = rows_of(coil)

    def scatter(phase, p):
        copies = []
        for distance in range(1, coils):
            target = lax.rem(coil + distance, coils)
            copies.append(
                pltpu.make_async_remote_copy(
                    src_ref=part.at[phase, :, p, rows_of(target)],
                    dst_ref=arrived.at[phase, distance - 1, :, p],
                    send_sem=block_send.at[2 * phase, p, distance - 1],
                    recv_sem=block_recv.at[2 * phase, p, distance - 1],
                    device_id=(slab, target),
                    device_id_type=MESH,
                )
            )
        for copy in copies:
            copy.start()
        return copies

    def gather(buffer, phase, p):
        copies = []
        for distance in range(1, coils):
            copies.append(
                pltpu.make_async_remote_copy(
                    src_ref=buffer.at[:, p, mine],
                    dst_ref=buffer.at[:, p, mine],
                    send_sem=block_send.at[2 * phase + 1, p, distance - 1],
                    recv_sem=block_recv.at[2 * phase + 1, p, distance - 1],
                    device_id=(slab, lax.rem(coil + distance, coils)),
                    device_id_type=MESH,
                )
            )
        for copy in copies:
            copy.start()
        return copies

    def tell(phase):
        copies = []
        for distance in range(1, devices):
            copies.append(
                pltpu.make_async_remote_copy(
                    src_ref=note.at[phase],
                    dst_ref=notes.at[phase, distance - 1],
                    send_sem=note_send.at[phase, distance - 1],
                    recv_sem=note_recv.at[phase, distance - 1],
                    device_id=device_at(distance),
                    device_id_type=MESH,
                )
            )
        for copy in copies:
            copy.start()
        return copies

    def finish(copies):
        for copy in copies:
            copy.wait()

    lanes = lax.broadcasted_iota(jnp.int32, (1, note.shape[2]), 1)

    def write_note(phase, values):
        line = jnp.zeros(lanes.shape, jnp.float32)
        for index, value in enumerate(values):
            line = jnp.where(lanes == index, value, line)
        note[phase] = line

    def read_notes(phase, count):
        line = note[phase]
        for distance in range(1, devices):
            line = line + notes[phase, distance - 1]
        return [jnp.sum(jnp.where(lanes == index, line, 0.0), axis=1, keepdims=True) for index in range(count)]

    def backward_part(real, imag, phase, p):
        imag, real = transform(imag, real, *tables)
        part[phase, 0, p] = maps[0, p] * real + maps[1, p] * imag
        part[phase, 1, p] = maps[0, p] * imag - maps[1, p] * real

    def forward(image_re, image_im, p):
        real = maps[0, p] * image_re - maps[1, p] * image_im
        imag = maps[0, p] * image_im + maps[1, p] * image_re
        real, imag = transform(real, imag, *tables)
        sampled = mask[p].astype(jnp.float32)
        return real * sampled, imag * sampled

    def reduced(phase, h, p):
        value = part[phase, h, p, mine]
        for distance in range(1, coils):
            value = value + arrived[phase, distance - 1, h, p]
        return value

    pending = []
    for p in range(planes):
        sampled = mask[p].astype(jnp.float32)
        backward_part(measured[0, p] * sampled, measured[1, p] * sampled, 0, p)
        pending.append(scatter(0, p))
    gathers = []
    norm = jnp.zeros((1, 1), jnp.float32)
    for p in range(planes):
        finish(pending[p])
        for h in range(2):
            value = reduced(0, h, p) + LAMBDA * prior[h, p]
            rhs[h, p, mine] = value
            norm = norm + total_of(value * value)
        gathers.append(gather(rhs, 0, p))
    energy = LAMBDA * norm
    pending = []
    for p in range(planes):
        finish(gathers[p])
        result = forward(rhs[0, p], rhs[1, p], p)
        for h in range(2):
            spectrum[h, p] = result[h]
            energy = energy + total_of(result[h] * result[h])
        if p == planes - 1:
            write_note(0, [norm, energy])
            first_notes = tell(0)
        backward_part(spectrum[0, p], spectrum[1, p], 1, p)
        pending.append(scatter(1, p))
    finish(first_notes)
    norm, curvature = read_notes(0, 2)
    step = norm / curvature
    gathers = []
    norm_next = jnp.zeros((1, 1), jnp.float32)
    cross = jnp.zeros((1, 1), jnp.float32)
    for p in range(planes):
        finish(pending[p])
        for h in range(2):
            direction = rhs[h, p, mine]
            value = direction - step * (reduced(1, h, p) + LAMBDA * direction)
            own_residual[h, p] = value
            residual[h, p, mine] = value.astype(jnp.bfloat16)
            norm_next = norm_next + total_of(value * value)
            cross = cross + LAMBDA * total_of(value * direction)
        gathers.append(gather(residual, 1, p))
    energy = LAMBDA * norm_next
    for p in range(planes):
        finish(gathers[p])
        result = forward(residual[0, p].astype(jnp.float32), residual[1, p].astype(jnp.float32), p)
        for h in range(2):
            energy = energy + total_of(result[h] * result[h])
            cross = cross + total_of(result[h] * spectrum[h, p])
    write_note(1, [norm_next, energy, cross])
    finish(tell(1))
    norm_next, energy, cross = read_notes(1, 3)
    ratio = norm_next / norm
    curvature = energy + 2.0 * ratio * cross + ratio * ratio * curvature
    step_next = norm_next / curvature
    for h in range(2):
        for p in range(planes):
            direction = rhs[h, p, mine]
            out[h, p] = step * direction + step_next * (own_residual[h, p] + ratio * direction)


def gradients(maps, measured, mask, prior):
    planes, rows, width = mask.shape
    block = prior.shape[2]
    shares = lax.axis_size("slab")
    coils = lax.axis_size("coil")
    cosine, sine = dft_parts(rows)
    y_tables = halves(np.concatenate([cosine, sine]))
    cosine, sine = dft_parts(width)
    z_tables = halves(np.block([[cosine, -sine], [sine, cosine]]))
    image = (2, planes, rows, width)
    brick = (2, planes, block, width)
    return pl.pallas_call(
        functools.partial(gradients_kernel, shares, coils),
        out_shape=jax.ShapeDtypeStruct(brick, jnp.float32),
        in_specs=[pl.BlockSpec(memory_space=pltpu.VMEM)] * 8,
        out_specs=pl.BlockSpec(memory_space=pltpu.VMEM),
        scratch_shapes=[
            pltpu.VMEM((2,) + image, jnp.float32),
            pltpu.VMEM((2, coils - 1) + brick, jnp.float32),
            pltpu.VMEM(image, jnp.float32),
            pltpu.VMEM(image, jnp.float32),
            pltpu.VMEM(brick, jnp.float32),
            pltpu.VMEM(image, jnp.bfloat16),
            pltpu.VMEM((2, 1, 128), jnp.float32),
            pltpu.VMEM((2, shares * coils - 1, 1, 128), jnp.float32),
            pltpu.SemaphoreType.DMA((4, planes, coils - 1)),
            pltpu.SemaphoreType.DMA((4, planes, coils - 1)),
            pltpu.SemaphoreType.DMA((2, shares * coils - 1)),
            pltpu.SemaphoreType.DMA((2, shares * coils - 1)),
        ],
        compiler_params=pltpu.CompilerParams(
            collective_id=0, has_side_effects=True, vmem_limit_bytes=56 * 1024 * 1024
        ),
    )(maps, measured, mask, prior, *y_tables, *z_tables)


def row_halo(cells, width):
    count = lax.axis_size("coil")
    tail = cells[:, :, cells.shape[2] - width :]
    head = cells[:, :, :width]
    return jnp.concatenate(
        [
            lax.ppermute(tail, "coil", [(i, i + 1) for i in range(count - 1)]),
            cells,
            lax.ppermute(head, "coil", [(i + 1, i) for i in range(count - 1)]),
        ],
        axis=2,
    )


def block_weights(weight, x_outs, y_outs, in_pad, out_pad):
    weight = jnp.pad(weight, ((0, out_pad), (0, in_pad), (0, 0), (0, 0), (0, 0)))
    weight = jnp.transpose(weight, (4, 0, 3, 2, 1))
    parts = []
    for x_out in range(x_outs):
        for y_out in range(y_outs):
            spread = ((0, 0), (0, 0), (y_out, y_outs - 1 - y_out), (x_out, x_outs - 1 - x_out), (0, 0))
            parts.append(jnp.pad(weight, spread))
    stacked = jnp.stack(parts)
    return stacked.reshape(stacked.shape[0] * stacked.shape[1] * stacked.shape[2], -1)


def conv_rows(weight_ref, source, sink, rows, planes, x_outs, y_outs, group, top, height, last):
    width = source.shape[-1]
    channels = source.shape[2]
    weight_rows = weight_ref.shape[0]
    outs = weight_rows // (3 * x_outs * y_outs)
    lanes = lax.broadcasted_iota(jnp.int32, (outs, width), 1)
    depth = (y_outs + 2) * (x_outs + 2) * channels

    def step(index, carry):
        y = index * y_outs
        for first in range(0, planes, x_outs * group):
            blocks = [
                source[pl.ds(y, y_outs + 2), first + k * x_outs : first + (k + 1) * x_outs + 2].reshape(depth, width)
                for k in range(group)
            ]
            taken = jnp.concatenate(blocks, axis=1) if group > 1 else blocks[0]
            product = jnp.dot(weight_ref[...], taken, preferred_element_type=jnp.float32)
            for x_out in range(x_outs):
                for y_out in range(y_outs):
                    base = (x_out * y_outs + y_out) * 3 * outs
                    y_now = y + y_out
                    inside = jnp.logical_and(top + y_now >= 0, top + y_now < height)
                    for k in range(group):
                        span = slice(k * width, (k + 1) * width)
                        before = product[base : base + outs, span]
                        centre = product[base + outs : base + 2 * outs, span]
                        after = product[base + 2 * outs : base + 3 * outs, span]
                        before = jnp.where(lanes == 0, 0.0, pltpu.roll(before, 1, 1))
                        after = jnp.where(lanes == width - 1, 0.0, pltpu.roll(after, width - 1, 1))
                        value = centre + before + after
                        plane = first + k * x_outs + x_out
                        if last:
                            sink[y_now, plane] = value
                        else:
                            value = jnp.where(inside, jnp.maximum(value, 0.0), 0.0)
                            sink[y_now, plane + 1] = value.astype(jnp.bfloat16)
        return carry

    lax.fori_loop(0, rows // y_outs, step, 0)


def spread_weights(taps, wide, x_outs, y_outs):
    count, channels = taps.shape[2:]
    span = (x_outs + 2) * channels
    empty = jnp.zeros((count, channels), taps.dtype)
    for x_out in range(x_outs):
        for y_out in range(y_outs):
            base = (x_out * y_outs + y_out) * count
            for y_in in range(y_outs + 2):
                tap = y_in - y_out
                if 0 <= tap < 3:
                    shifts = [x_in - x_out for x_in in range(x_outs + 2)]
                    pieces = [taps[u, tap] if 0 <= u < 3 else empty for u in shifts]
                    block = jnp.concatenate(pieces, axis=1)
                else:
                    block = jnp.zeros((count, span), taps.dtype)
                wide[base : base + count, y_in * span : (y_in + 1) * span] = block


def denoise_kernel(
    x_outs, y_outs, group, rows, block_rows, height, features, first, middle, final, out, even, odd, wide
):
    planes = features.shape[1] - 2
    layers = middle.shape[0] + 2
    top = lax.axis_index("coil") * block_rows + lax.axis_index("slab") * rows
    buffers = (even, odd)
    for buffer in buffers:
        edge = jnp.zeros((buffer.shape[0],) + buffer.shape[2:], buffer.dtype)
        buffer[:, 0] = edge
        buffer[:, planes + 1] = edge
    shared = (planes, x_outs, y_outs, group)
    left = layers - 1
    for layer in range(layers - 2):
        spread_weights(middle.at[layer], wide.at[layer], x_outs, y_outs)
    conv_rows(first, features, even, rows + 2 * left, *shared, top - left, height, False)
    for layer in range(layers - 2):
        left = left - 1
        conv_rows(
            wide.at[layer], buffers[layer % 2], buffers[(layer + 1) % 2],
            rows + 2 * left, *shared, top - left, height, False,
        )
    conv_rows(final, buffers[(layers - 2) % 2], out, rows, *shared, top, height, True)


def denoise(features, w_first, w_middle, w_last, rows, block_rows, height):
    planes = features.shape[1]
    width = features.shape[3]
    channels = w_first.shape[0]
    layers = w_middle.shape[0] + 2
    x_outs = 2 if planes % 2 == 0 else 1
    y_outs = 2 if rows % 2 == 0 else 1
    group = 2 if (planes // x_outs) % 2 == 0 else 1
    in_rows = 16
    features = jnp.pad(features, ((0, 0), (1, 1), (0, in_rows - features.shape[2]), (0, 0)))
    first = block_weights(w_first, x_outs, y_outs, in_rows - w_first.shape[1], 0)
    middle = jnp.transpose(w_middle, (0, 3, 4, 5, 1, 2)).reshape(layers - 2, 3, 3, 3 * channels, channels)
    wide = (layers - 2, x_outs * y_outs * 3 * channels, (x_outs + 2) * (y_outs + 2) * channels)
    final = block_weights(w_last, x_outs, y_outs, 0, -w_last.shape[0] % 8)
    outs = w_last.shape[0]
    held = (rows + 2 * (layers - 1), planes + 2, channels, width)
    result = pl.pallas_call(
        functools.partial(denoise_kernel, x_outs, y_outs, group, rows, block_rows, height),
        out_shape=jax.ShapeDtypeStruct((rows, planes, outs + -outs % 8, width), jnp.float32),
        in_specs=[pl.BlockSpec(memory_space=pltpu.VMEM)] * 4,
        out_specs=pl.BlockSpec(memory_space=pltpu.VMEM),
        scratch_shapes=[pltpu.VMEM(dims, jnp.bfloat16) for dims in (held, held, wide)],
        compiler_params=pltpu.CompilerParams(vmem_limit_bytes=48 * 1024 * 1024),
    )(features, first, middle, final)
    return result[:, :, :outs]


def body(sensitivity, kspace, sampling, prior_image, w_first, w_middle, w_last):
    brick = gradients(sensitivity[0], kspace[0], sampling, prior_image)
    len_y = sampling.shape[1]
    block_rows = prior_image.shape[2]
    halo = w_middle.shape[0] + 2
    shares = lax.axis_size("slab")
    rows = block_rows // shares
    mine = row_halo(brick.astype(jnp.bfloat16), halo)
    mine = jnp.transpose(mine, (2, 1, 0, 3))
    pieces = jnp.stack([mine[s * rows : (s + 1) * rows + 2 * halo] for s in range(shares)])
    taken = lax.all_to_all(pieces, "slab", 0, 0)
    features = jnp.moveaxis(taken, 0, 1).reshape((rows + 2 * halo, -1) + taken.shape[3:])
    correction = denoise(features, w_first, w_middle, w_last, rows, block_rows, len_y)
    local = prior_image.shape[1]
    pieces = jnp.moveaxis(correction.reshape((rows, shares, local) + correction.shape[2:]), 1, 0)
    taken = lax.all_to_all(pieces, "slab", 0, 0)
    correction = jnp.transpose(taken.reshape((block_rows,) + taken.shape[2:]), (2, 1, 0, 3))
    return (brick, brick + correction)


def solution(mesh):
    placed = (
        P("coil", None, "slab", None, None),
        P("coil", None, "slab", None, None),
        P("slab", None, None),
        P(None, "slab", "coil", None),
        P(),
        P(),
        P(),
    )
    return jax.shard_map(
        body,
        mesh=mesh,
        in_specs=placed,
        out_specs=(P(None, "slab", "coil", None), P(None, "slab", "coil", None)),
        check_vma=False,
    )
```

```python
import functools

import jax
import jax.numpy as jnp
import numpy as np
from jax import lax
from jax.experimental import pallas as pl
from jax.experimental.pallas import tpu as pltpu
from jax.sharding import PartitionSpec as P

LAMBDA = 0.5
MESH = pl.DeviceIdType.MESH


def dft_parts(length):
    positions = np.arange(length)
    angles = 2.0 * np.pi / length * (positions[:, None] * positions[None, :] % length)
    return np.cos(angles) / np.sqrt(length), np.sin(angles) / np.sqrt(length)


def halves(table):
    table = table.astype(np.float32)
    high = table.astype(jnp.bfloat16)
    low = (table - high.astype(np.float32)).astype(jnp.bfloat16)
    return jnp.asarray(high), jnp.asarray(low)


def split(values):
    high = values.astype(jnp.bfloat16)
    return high, (values - high.astype(jnp.float32)).astype(jnp.bfloat16)


def multiply(left, right):
    return jnp.dot(left, right, preferred_element_type=jnp.float32)


def transform(real, imag, y_high, y_low, z_high, z_low):
    rows, width = real.shape
    high, low = split(jnp.concatenate([real, imag], axis=1))
    both = multiply(y_high[...], jnp.concatenate([high, low], axis=1))
    field = both[:, : 2 * width] + both[:, 2 * width :] + multiply(y_low[...], high)
    field = jnp.concatenate(
        [field[:rows, :width] + field[rows:, width:], field[:rows, width:] - field[rows:, :width]], axis=1
    )
    high, low = split(field)
    both = multiply(jnp.concatenate([high, low], axis=0), z_high[...])
    field = both[:rows] + both[rows:] + multiply(high, z_low[...])
    return field[:, :width], field[:, width:]


def total_of(values):
    return jnp.sum(jnp.sum(values, axis=0, keepdims=True), axis=1, keepdims=True)


def gradients_kernel(
    shares, coils, maps, measured, mask, prior, y_high, y_low, z_high, z_low,
    out, beside, part, arrived, rhs, spectrum, own_residual, residual, note, notes, edges,
    block_send, block_recv, note_send, note_recv, edge_send, edge_recv,
):
    slab = lax.axis_index("slab")
    coil = lax.axis_index("coil")
    devices = shares * coils
    me = slab * coils + coil
    planes = maps.shape[1]
    block = prior.shape[2]
    tables = (y_high, y_low, z_high, z_low)

    def device_at(distance):
        other = lax.rem(me + distance, devices)
        return (other // coils, lax.rem(other, coils))

    barrier = pltpu.get_barrier_semaphore()
    for distance in range(1, devices):
        pl.semaphore_signal(barrier, inc=1, device_id=device_at(distance), device_id_type=MESH)
    pl.semaphore_wait(barrier, devices - 1)

    def rows_of(index):
        return pl.ds(pl.multiple_of(index * block, block), block)

    mine = rows_of(coil)

    def scatter(phase, p):
        copies = []
        for distance in range(1, coils):
            target = lax.rem(coil + distance, coils)
            copies.append(
                pltpu.make_async_remote_copy(
                    src_ref=part.at[phase, :, p, rows_of(target)],
                    dst_ref=arrived.at[phase, distance - 1, :, p],
                    send_sem=block_send.at[2 * phase, p, distance - 1],
                    recv_sem=block_recv.at[2 * phase, p, distance - 1],
                    device_id=(slab, target),
                    device_id_type=MESH,
                )
            )
        for copy in copies:
            copy.start()
        return copies

    def gather(buffer, phase, p):
        copies = []
        for distance in range(1, coils):
            copies.append(
                pltpu.make_async_remote_copy(
                    src_ref=buffer.at[:, p, mine],
                    dst_ref=buffer.at[:, p, mine],
                    send_sem=block_send.at[2 * phase + 1, p, distance - 1],
                    recv_sem=block_recv.at[2 * phase + 1, p, distance - 1],
                    device_id=(slab, lax.rem(coil + distance, coils)),
                    device_id_type=MESH,
                )
            )
        for copy in copies:
            copy.start()
        return copies

    def tell(phase):
        copies = []
        for distance in range(1, devices):
            copies.append(
                pltpu.make_async_remote_copy(
                    src_ref=note.at[phase],
                    dst_ref=notes.at[phase, distance - 1],
                    send_sem=note_send.at[phase, distance - 1],
                    recv_sem=note_recv.at[phase, distance - 1],
                    device_id=device_at(distance),
                    device_id_type=MESH,
                )
            )
        for copy in copies:
            copy.start()
        return copies

    margin = edges.shape[3]
    above = lax.rem(coil + coils - 1, coils)
    below = lax.rem(coil + 1, coils)

    def send_edges(p):
        copies = []
        for side, first, target in ((0, block - margin, below), (1, 0, above)):
            copies.append(
                pltpu.make_async_remote_copy(
                    src_ref=own_residual.at[:, p, first : first + margin],
                    dst_ref=edges.at[side, :, p],
                    send_sem=edge_send.at[side, p],
                    recv_sem=edge_recv.at[side, p],
                    device_id=(slab, target),
                    device_id_type=MESH,
                )
            )
        for copy in copies:
            copy.start()
        return copies

    def finish(copies):
        for copy in copies:
            copy.wait()

    lanes = lax.broadcasted_iota(jnp.int32, (1, note.shape[2]), 1)

    def write_note(phase, values):
        line = jnp.zeros(lanes.shape, jnp.float32)
        for index, value in enumerate(values):
            line = jnp.where(lanes == index, value, line)
        note[phase] = line

    def read_notes(phase, count):
        line = note[phase]
        for distance in range(1, devices):
            line = line + notes[phase, distance - 1]
        return [jnp.sum(jnp.where(lanes == index, line, 0.0), axis=1, keepdims=True) for index in range(count)]

    def backward_part(real, imag, phase, p):
        imag, real = transform(imag, real, *tables)
        part[phase, 0, p] = maps[0, p] * real + maps[1, p] * imag
        part[phase, 1, p] = maps[0, p] * imag - maps[1, p] * real

    def forward(image_re, image_im, p):
        real = maps[0, p] * image_re - maps[1, p] * image_im
        imag = maps[0, p] * image_im + maps[1, p] * image_re
        real, imag = transform(real, imag, *tables)
        sampled = mask[p].astype(jnp.float32)
        return real * sampled, imag * sampled

    def reduced(phase, h, p):
        value = part[phase, h, p, mine]
        for distance in range(1, coils):
            value = value + arrived[phase, distance - 1, h, p]
        return value

    pending = []
    for p in range(planes):
        sampled = mask[p].astype(jnp.float32)
        backward_part(measured[0, p] * sampled, measured[1, p] * sampled, 0, p)
        pending.append(scatter(0, p))
    gathers = []
    norm = jnp.zeros((1, 1), jnp.float32)
    for p in range(planes):
        finish(pending[p])
        for h in range(2):
            value = reduced(0, h, p) + LAMBDA * prior[h, p]
            rhs[h, p, mine] = value
            norm = norm + total_of(value * value)
        gathers.append(gather(rhs, 0, p))
    energy = LAMBDA * norm
    pending = []
    for p in range(planes):
        finish(gathers[p])
        result = forward(rhs[0, p], rhs[1, p], p)
        for h in range(2):
            spectrum[h, p] = result[h]
            energy = energy + total_of(result[h] * result[h])
        if p == planes - 1:
            write_note(0, [norm, energy])
            first_notes = tell(0)
        backward_part(spectrum[0, p], spectrum[1, p], 1, p)
        pending.append(scatter(1, p))
    finish(first_notes)
    norm, curvature = read_notes(0, 2)
    step = norm / curvature
    gathers = []
    norm_next = jnp.zeros((1, 1), jnp.float32)
    cross = jnp.zeros((1, 1), jnp.float32)
    for p in range(planes):
        finish(pending[p])
        for h in range(2):
            direction = rhs[h, p, mine]
            value = direction - step * (reduced(1, h, p) + LAMBDA * direction)
            own_residual[h, p] = value
            residual[h, p, mine] = value.astype(jnp.bfloat16)
            norm_next = norm_next + total_of(value * value)
            cross = cross + LAMBDA * total_of(value * direction)
        gathers.append(gather(residual, 1, p) + send_edges(p))
    energy = LAMBDA * norm_next
    for p in range(planes):
        finish(gathers[p])
        result = forward(residual[0, p].astype(jnp.float32), residual[1, p].astype(jnp.float32), p)
        for h in range(2):
            energy = energy + total_of(result[h] * result[h])
            cross = cross + total_of(result[h] * spectrum[h, p])
    write_note(1, [norm_next, energy, cross])
    finish(tell(1))
    norm_next, energy, cross = read_notes(1, 3)
    ratio = norm_next / norm
    curvature = energy + 2.0 * ratio * cross + ratio * ratio * curvature
    step_next = norm_next / curvature
    for h in range(2):
        for p in range(planes):
            direction = rhs[h, p, mine]
            out[h, p] = step * direction + step_next * (own_residual[h, p] + ratio * direction)
            for side, start, inside in (
                (0, above * block + block - margin, coil > 0), (1, below * block, coil < coils - 1)
            ):
                direction = rhs[h, p, pl.ds(pl.multiple_of(start, margin), margin)]
                value = step * direction + step_next * (edges[side, h, p] + ratio * direction)
                beside[side, h, p] = jnp.where(inside, value, 0.0)


def gradients(maps, measured, mask, prior, margin):
    planes, rows, width = mask.shape
    block = prior.shape[2]
    shares = lax.axis_size("slab")
    coils = lax.axis_size("coil")
    cosine, sine = dft_parts(rows)
    y_tables = halves(np.concatenate([cosine, sine]))
    cosine, sine = dft_parts(width)
    z_tables = halves(np.block([[cosine, -sine], [sine, cosine]]))
    image = (2, planes, rows, width)
    brick = (2, planes, block, width)
    margins = (2, 2, planes, margin, width)
    return pl.pallas_call(
        functools.partial(gradients_kernel, shares, coils),
        out_shape=[jax.ShapeDtypeStruct(dims, jnp.float32) for dims in (brick, margins)],
        in_specs=[pl.BlockSpec(memory_space=pltpu.VMEM)] * 8,
        out_specs=[pl.BlockSpec(memory_space=pltpu.VMEM)] * 2,
        scratch_shapes=[
            pltpu.VMEM((2,) + image, jnp.float32),
            pltpu.VMEM((2, coils - 1) + brick, jnp.float32),
            pltpu.VMEM(image, jnp.float32),
            pltpu.VMEM(image, jnp.float32),
            pltpu.VMEM(brick, jnp.float32),
            pltpu.VMEM(image, jnp.bfloat16),
            pltpu.VMEM((2, 1, 128), jnp.float32),
            pltpu.VMEM((2, shares * coils - 1, 1, 128), jnp.float32),
            pltpu.VMEM(margins, jnp.float32),
            pltpu.SemaphoreType.DMA((4, planes, coils - 1)),
            pltpu.SemaphoreType.DMA((4, planes, coils - 1)),
            pltpu.SemaphoreType.DMA((2, shares * coils - 1)),
            pltpu.SemaphoreType.DMA((2, shares * coils - 1)),
            pltpu.SemaphoreType.DMA((2, planes)),
            pltpu.SemaphoreType.DMA((2, planes)),
        ],
        compiler_params=pltpu.CompilerParams(
            collective_id=0, has_side_effects=True, vmem_limit_bytes=56 * 1024 * 1024
        ),
    )(maps, measured, mask, prior, *y_tables, *z_tables)


def block_weights(weight, x_outs, y_outs, in_pad, out_pad):
    weight = jnp.pad(weight, ((0, out_pad), (0, in_pad), (0, 0), (0, 0), (0, 0)))
    weight = jnp.transpose(weight, (4, 0, 3, 2, 1))
    parts = []
    for x_out in range(x_outs):
        for y_out in range(y_outs):
            spread = ((0, 0), (0, 0), (y_out, y_outs - 1 - y_out), (x_out, x_outs - 1 - x_out), (0, 0))
            parts.append(jnp.pad(weight, spread))
    stacked = jnp.stack(parts)
    return stacked.reshape(stacked.shape[0] * stacked.shape[1] * stacked.shape[2], -1)


def conv_rows(weight_ref, source, sink, rows, planes, x_outs, y_outs, group, top, height, last):
    width = source.shape[-1]
    channels = source.shape[2]
    weight_rows = weight_ref.shape[0]
    outs = weight_rows // (3 * x_outs * y_outs)
    lanes = lax.broadcasted_iota(jnp.int32, (outs, width), 1)
    depth = (y_outs + 2) * (x_outs + 2) * channels

    def step(index, carry):
        y = index * y_outs
        for first in range(0, planes, x_outs * group):
            blocks = [
                source[pl.ds(y, y_outs + 2), first + k * x_outs : first + (k + 1) * x_outs + 2].reshape(depth, width)
                for k in range(group)
            ]
            taken = jnp.concatenate(blocks, axis=1) if group > 1 else blocks[0]
            product = jnp.dot(weight_ref[...], taken, preferred_element_type=jnp.float32)
            for x_out in range(x_outs):
                for y_out in range(y_outs):
                    base = (x_out * y_outs + y_out) * 3 * outs
                    y_now = y + y_out
                    inside = jnp.logical_and(top + y_now >= 0, top + y_now < height)
                    for k in range(group):
                        span = slice(k * width, (k + 1) * width)
                        before = product[base : base + outs, span]
                        centre = product[base + outs : base + 2 * outs, span]
                        after = product[base + 2 * outs : base + 3 * outs, span]
                        before = jnp.where(lanes == 0, 0.0, pltpu.roll(before, 1, 1))
                        after = jnp.where(lanes == width - 1, 0.0, pltpu.roll(after, width - 1, 1))
                        value = centre + before + after
                        plane = first + k * x_outs + x_out
                        if last:
                            sink[y_now, plane] = value
                        else:
                            value = jnp.where(inside, jnp.maximum(value, 0.0), 0.0)
                            sink[y_now, plane + 1] = value.astype(jnp.bfloat16)
        return carry

    lax.fori_loop(0, rows // y_outs, step, 0)


def spread_weights(taps, wide, x_outs, y_outs):
    count, channels = taps.shape[2:]
    span = (x_outs + 2) * channels
    empty = jnp.zeros((count, channels), taps.dtype)
    for x_out in range(x_outs):
        for y_out in range(y_outs):
            base = (x_out * y_outs + y_out) * count
            for y_in in range(y_outs + 2):
                tap = y_in - y_out
                if 0 <= tap < 3:
                    shifts = [x_in - x_out for x_in in range(x_outs + 2)]
                    pieces = [taps[u, tap] if 0 <= u < 3 else empty for u in shifts]
                    block = jnp.concatenate(pieces, axis=1)
                else:
                    block = jnp.zeros((count, span), taps.dtype)
                wide[base : base + count, y_in * span : (y_in + 1) * span] = block


def denoise_kernel(
    x_outs, y_outs, group, rows, block_rows, height, features, first, middle, final, out, even, odd, wide
):
    planes = features.shape[1] - 2
    layers = middle.shape[0] + 2
    top = lax.axis_index("coil") * block_rows + lax.axis_index("slab") * rows
    buffers = (even, odd)
    for buffer in buffers:
        edge = jnp.zeros((buffer.shape[0],) + buffer.shape[2:], buffer.dtype)
        buffer[:, 0] = edge
        buffer[:, planes + 1] = edge
    shared = (planes, x_outs, y_outs, group)
    left = layers - 1
    for layer in range(layers - 2):
        spread_weights(middle.at[layer], wide.at[layer], x_outs, y_outs)
    conv_rows(first, features, even, rows + 2 * left, *shared, top - left, height, False)
    for layer in range(layers - 2):
        left = left - 1
        conv_rows(
            wide.at[layer], buffers[layer % 2], buffers[(layer + 1) % 2],
            rows + 2 * left, *shared, top - left, height, False,
        )
    conv_rows(final, buffers[(layers - 2) % 2], out, rows, *shared, top, height, True)


def denoise(features, w_first, w_middle, w_last, rows, block_rows, height):
    planes = features.shape[1]
    width = features.shape[3]
    channels = w_first.shape[0]
    layers = w_middle.shape[0] + 2
    x_outs = 2 if planes % 2 == 0 else 1
    y_outs = 2 if rows % 2 == 0 else 1
    group = 2 if (planes // x_outs) % 2 == 0 else 1
    in_rows = 16
    features = jnp.pad(features, ((0, 0), (1, 1), (0, in_rows - features.shape[2]), (0, 0)))
    first = block_weights(w_first, x_outs, y_outs, in_rows - w_first.shape[1], 0)
    middle = jnp.transpose(w_middle, (0, 3, 4, 5, 1, 2)).reshape(layers - 2, 3, 3, 3 * channels, channels)
    wide = (layers - 2, x_outs * y_outs * 3 * channels, (x_outs + 2) * (y_outs + 2) * channels)
    final = block_weights(w_last, x_outs, y_outs, 0, -w_last.shape[0] % 8)
    outs = w_last.shape[0]
    held = (rows + 2 * (layers - 1), planes + 2, channels, width)
    result = pl.pallas_call(
        functools.partial(denoise_kernel, x_outs, y_outs, group, rows, block_rows, height),
        out_shape=jax.ShapeDtypeStruct((rows, planes, outs + -outs % 8, width), jnp.float32),
        in_specs=[pl.BlockSpec(memory_space=pltpu.VMEM)] * 4,
        out_specs=pl.BlockSpec(memory_space=pltpu.VMEM),
        scratch_shapes=[pltpu.VMEM(dims, jnp.bfloat16) for dims in (held, held, wide)],
        compiler_params=pltpu.CompilerParams(vmem_limit_bytes=48 * 1024 * 1024),
    )(features, first, middle, final)
    return result[:, :, :outs]


def body(sensitivity, kspace, sampling, prior_image, w_first, w_middle, w_last):
    halo = w_middle.shape[0] + 2
    margin = halo + -halo % 8
    brick, beside = gradients(sensitivity[0], kspace[0], sampling, prior_image, margin)
    len_y = sampling.shape[1]
    block_rows = prior_image.shape[2]
    shares = lax.axis_size("slab")
    rows = block_rows // shares
    mine = jnp.concatenate([beside[0, :, :, margin - halo :], brick, beside[1, :, :, :halo]], axis=2)
    mine = mine.astype(jnp.bfloat16)
    mine = jnp.transpose(mine, (2, 1, 0, 3))
    pieces = jnp.stack([mine[s * rows : (s + 1) * rows + 2 * halo] for s in range(shares)])
    taken = lax.all_to_all(pieces, "slab", 0, 0)
    features = jnp.moveaxis(taken, 0, 1).reshape((rows + 2 * halo, -1) + taken.shape[3:])
    correction = denoise(features, w_first, w_middle, w_last, rows, block_rows, len_y)
    local = prior_image.shape[1]
    pieces = jnp.moveaxis(correction.reshape((rows, shares, local) + correction.shape[2:]), 1, 0)
    taken = lax.all_to_all(pieces, "slab", 0, 0)
    correction = jnp.transpose(taken.reshape((block_rows,) + taken.shape[2:]), (2, 1, 0, 3))
    return (brick, brick + correction)


def solution(mesh):
    placed = (
        P("coil", None, "slab", None, None),
        P("coil", None, "slab", None, None),
        P("slab", None, None),
        P(None, "slab", "coil", None),
        P(),
        P(),
        P(),
    )
    return jax.shard_map(
        body,
        mesh=mesh,
        in_specs=placed,
        out_specs=(P(None, "slab", "coil", None), P(None, "slab", "coil", None)),
        check_vma=False,
    )
```
